128 devices in a mesh: chan: 8 (over x, z_hi), row: 4 (over y), col: 4 (over z_lo, core).
Axes of the slice: x: 4, y: 4, z: 4 (z_hi: 2, z_lo: 2; z = z_hi * 2 + z_lo), core: 2. Of those that a mesh axis runs over, the one named last changes fastest.
Arguments:
- voltages: bfloat16 [2, 4, 512, 64, 1031], P(None, None, ('chan', 'row', 'col')), may hold values from -6 to 6
- window: float32 [8, 64], replicated, may hold values from 0.1 to 0.6
- kept_channels: int32 [48], replicated, may hold values from 0 to 63, as said below
Outputs:
- covariance: float32 [48, 2, 2048, 2048], P('chan', None, 'row', 'col')
The draws below stay inside these ranges and needn't reach their ends.
Inputs may be any that keep to these rules, and one draw needn't show every extreme that they name: `kept_channels`: 48 distinct channel numbers of the 64-point transform, in any order.
All inputs are finite; a program needn't handle non-finite values.
Results may differ from the reference program's by a relative error of at most 0.0019.
Values may be sent and summed in bfloat16 or wider, within the bound.
No kernel may reach another device: no remote copies, remote signals or barrier semaphores. Data moves between devices by JAX's collectives and lax.ppermute only.
A program may use at most 128 MiB of HBM per device.

```python
import math
import jax
import jax.numpy as jnp
from jax import lax

NIN = 2048
POINTS = 64
KEEP = 48
TAPS = 8
FRAMES = 1024
BLOCKS = 1031
PANEL = 512
N_ROW = 4


def draw_kept_channels(key, part):
    return jax.random.permutation(key, POINTS)[:KEEP].astype(jnp.int32)


def steps_of(own_key, shape, shards, smallest, largest):
    level, own = 1.0, jax.random.fold_in(own_key, 6)
    for position, blocks in shards:
        steps = jnp.exp(jax.random.uniform(jax.random.fold_in(own, position), (blocks,), jnp.float32, smallest / len(shards), largest / len(shards)))
        level = level * jnp.repeat(steps, shape[position] // blocks).reshape([-1 if axis == position else 1 for axis in range(len(shape))])
    return level


def centred(rng, shape, deviation, bound, shards=(), held_as=jnp.bfloat16):
    loudness = steps_of(rng, shape, shards, -0.22, 0.18) if shards else 1.0
    result = jax.random.normal(rng, shape, jnp.float32) * deviation * loudness
    return jnp.minimum(jnp.maximum(result, -bound), bound).astype(held_as)


def setup_inputs(seed: int = 0) -> dict:
    seeds = jax.random.split(jax.random.key(seed), 4)
    voltages = centred(seeds[0], (2, N_ROW, PANEL, POINTS, BLOCKS), 1.0, 6.0, ((2, 128),))
    window = jnp.clip(jax.random.uniform(seeds[1], (TAPS, POINTS), jnp.float32, 0.1, 0.6), 0.1, 0.6)
    kept_channels = draw_kept_channels(jax.random.fold_in(seeds[3], 71), 0)
    return {"voltages": voltages, "window": window, "kept_channels": kept_channels}


def phase_table(kept_channels, points):
    positions = jnp.arange(points, dtype=jnp.int32)
    phases = kept_channels.astype(jnp.int32)[:, None] * positions[None, :] % points
    angles = phases.astype(jnp.float32) * (2.0 * math.pi / points)
    factor = 1.0 / math.sqrt(points)
    cosines = jnp.cos(angles) * factor
    sines = jnp.sin(angles) * factor
    return jnp.stack([jnp.stack([cosines, -sines]), jnp.stack([sines, cosines])])

def filter_bank(samples, window, frames):
    filtered = window[0][:, None] * samples[..., 0:frames]
    for tap_index in range(1, window.shape[0]):
        filtered = filtered + window[tap_index][:, None] * samples[..., tap_index:tap_index + frames]
    return filtered

def reference(voltages, window, kept_channels):
    samples = voltages.astype(jnp.float32).reshape(2, NIN, POINTS, BLOCKS)
    filtered = filter_bank(samples, window, FRAMES)
    table = phase_table(kept_channels, POINTS)
    spectra = jnp.einsum('qsnf,qpkn->kpsf', filtered, table, precision=lax.Precision.HIGHEST).astype(jnp.bfloat16)

    def correlate(spectrum):
        real_rows = spectrum[0]
        imag_rows = spectrum[1]
        stacked = jnp.concatenate([real_rows, imag_rows], axis=1)
        real_part = jnp.dot(stacked, stacked.T, preferred_element_type=jnp.float32)
        imag_part = jnp.dot(imag_rows, real_rows.T, preferred_element_type=jnp.float32)
        imag_part = imag_part - jnp.dot(real_rows, imag_rows.T, preferred_element_type=jnp.float32)
        return jnp.stack([real_part, imag_part]) * (1.0 / FRAMES)
    return lax.map(correlate, spectra)
```

```python
import functools
import math

import jax
import jax.numpy as jnp
from jax import lax
from jax.experimental import pallas as pl
from jax.experimental.pallas import tpu as pltpu
from jax.sharding import Mesh
from jax.sharding import PartitionSpec as P

CHAN_COL = ("chan", "col_0", "col_1")
CHAN_ROW_COL = ("chan", "row", "col_0", "col_1")
CHUNKS = 2
STEPS = (("row", (0,)), ("col", (0,)), ("row", (1,)), ("col", (1,)))
F32 = jnp.float32
BF16 = jnp.bfloat16


def split_bf16(x):
    hi = x.astype(BF16)
    return hi, (x - hi.astype(F32)).astype(BF16)


def phase_rows(kept_channels, points, chan_count, slots):
    positions = jnp.arange(points, dtype=jnp.int32)
    phases = kept_channels[:, None] * positions[None, :] % points
    angles = phases.astype(F32) * (2.0 * math.pi / points)
    factor = 1.0 / math.sqrt(points)
    cosines = jnp.cos(angles) * factor
    sines = jnp.sin(angles) * factor
    per_chan = kept_channels.shape[0] // chan_count
    real = jnp.concatenate([cosines, sines], axis=1)
    imag = jnp.concatenate([-sines, cosines], axis=1)
    rows = jnp.stack([real, imag], axis=1)
    rows = rows.reshape(chan_count, CHUNKS, per_chan // CHUNKS, 2, 2 * points)
    rows = rows.transpose(1, 0, 2, 3, 4).reshape(-1, 2 * points)
    eye = jnp.eye(slots, dtype=F32)
    blocks = rows[:, None, None, :] * eye[None, :, :, None]
    blocks = blocks.reshape(rows.shape[0] * slots, slots * 2 * points)
    near = lax.reduce_precision(blocks, 8, 7)
    return near.astype(BF16), (blocks - near).astype(BF16)


def spectra_kernel(volt_ref, win_ref, hi_ref, lo_ref, *refs):
    out_refs, part_ref = refs[:-1], refs[-1]
    slots, points, _ = volt_ref.shape[2:]
    frames = part_ref.shape[1]
    depth = slots * 2 * points
    group = 16
    steps = points // group

    def filter_rows(i, _):
        slot, plane, at = i // (2 * steps), i // steps % 2, i % steps * group
        x = volt_ref[plane, 0, slot, pl.ds(at, group), :]
        total = None
        for tap in range(win_ref.shape[0]):
            gain = win_ref[tap, pl.ds(at, group), :]
            gain = jnp.concatenate([gain] * (frames // 128), axis=1)
            term = gain * x[:, tap : tap + frames].astype(F32)
            total = term if total is None else total + term
        hi, lo = split_bf16(total)
        to = pl.multiple_of(i * group, group)
        part_ref[pl.ds(to, group)] = hi
        part_ref[pl.ds(to + depth, group)] = lo
        return 0

    lax.fori_loop(0, slots * 2 * steps, filter_rows, 0, unroll=4)
    out = jnp.dot(hi_ref[...], part_ref[0:depth], preferred_element_type=F32)
    out = out + jnp.dot(hi_ref[...], part_ref[depth:], preferred_element_type=F32)
    out = out + jnp.dot(lo_ref[...], part_ref[0:depth], preferred_element_type=F32)
    chans = out_refs[0].shape[0]
    out = out.astype(BF16).reshape(CHUNKS, chans, -1, frames)
    rows = out.shape[2]
    for (kind, pieces), ref in zip(STEPS, out_refs):
        for k, piece in enumerate(pieces):
            at = slice(k * rows, (k + 1) * rows)
            if kind == "col":
                ref[:, 0, at] = out[piece]
                continue
            quarter = ref.shape[4]
            for part in range(frames // quarter):
                ref[:, 0, part, at] = out[piece, :, :, part * quarter : (part + 1) * quarter]


def spectra(voltages, window, hi, lo, chan_count, col_count):
    _, panels, slots, points, blocks = voltages.shape
    taps = window.shape[0]
    frames = blocks - taps + 1
    rows = hi.shape[0] // (CHUNKS * chan_count)
    depth = hi.shape[1]
    width = pl.cdiv(blocks, 128) * 128
    window = jnp.broadcast_to(window[:, :, None], (taps, points, 128))
    quarter = frames // col_count
    specs, shapes = [], []
    for kind, pieces in STEPS:
        high = rows * len(pieces)
        inner = (high, frames) if kind == "col" else (col_count, high, quarter)
        zeros = (0,) * len(inner)
        specs.append(
            pl.BlockSpec((chan_count, 1, *inner), lambda p, zeros=zeros: (0, p, *zeros))
        )
        shapes.append(jax.ShapeDtypeStruct((chan_count, panels, *inner), BF16))
    return pl.pallas_call(
        spectra_kernel,
        grid=(panels,),
        in_specs=[
            pl.BlockSpec((2, 1, slots, points, width), lambda p: (0, p, 0, 0, 0)),
            pl.BlockSpec((taps, points, 128), lambda p: (0, 0, 0)),
            pl.BlockSpec(hi.shape, lambda p: (0, 0)),
            pl.BlockSpec(lo.shape, lambda p: (0, 0)),
        ],
        out_specs=specs,
        out_shape=shapes,
        scratch_shapes=[pltpu.VMEM((2 * depth, frames), BF16)],
        compiler_params=pltpu.CompilerParams(vmem_limit_bytes=48 << 20),
        name="spectra",
    )(voltages, window, hi, lo)


def regroup_kernel(size, slots, x_ref, *out_refs):
    kinds = out_refs[0].shape[0]
    total = kinds * len(out_refs)
    per = size // total
    rows = lax.broadcasted_iota(jnp.int32, (size, size), 0)
    cols = lax.broadcasted_iota(jnp.int32, (size, size), 1)
    kind, rest = rows // per, rows % per
    source = (rest // slots) * (total * slots) + kind * slots + rest % slots
    pick = (cols == source).astype(F32).astype(BF16)
    for g in range(x_ref.shape[0] // size):
        out = jnp.dot(
            pick, x_ref[g * size : (g + 1) * size], preferred_element_type=F32
        ).astype(BF16)
        out = out.reshape(total, per, -1)
        for k, ref in enumerate(out_refs):
            ref[:, g * per : (g + 1) * per] = out[k * kinds : (k + 1) * kinds]


def regroup(x, kinds, slots):
    count, rows, frames = x.shape
    pieces = rows // (kinds * slots)
    size = rows * (16 if pieces == 1 else 8)
    steps = 2
    part = count * rows // steps
    high = count * slots
    return pl.pallas_call(
        functools.partial(regroup_kernel, size, slots),
        grid=(steps,),
        in_specs=[pl.BlockSpec((part, frames), lambda g: (g, 0))],
        out_specs=[pl.BlockSpec((kinds, high // steps, frames), lambda g: (0, g, 0))] * pieces,
        out_shape=[jax.ShapeDtypeStruct((kinds, high, frames), BF16)] * pieces,
        cost_estimate=pl.CostEstimate(
            flops=2 * size * count * rows * frames,
            bytes_accessed=4 * count * rows * frames,
            transcendentals=0,
        ),
        compiler_params=pltpu.CompilerParams(vmem_limit_bytes=24 << 20),
        name="regroup",
    )(x.reshape(count * rows, frames))


def correlate_kernel(order_ref, *refs):
    cols, pieces = refs[0:4], refs[4:8]
    out_ref, a_ref, b_ref = refs[-3:]
    frames = cols[0].shape[4]
    quarter = pieces[0].shape[3]
    for plane in range(2):
        for k, ref in enumerate(cols):
            b_ref[:, order_ref[k], :, plane * frames : (plane + 1) * frames] = ref[0, plane]
        for k, ref in enumerate(pieces):
            at = pl.multiple_of(order_ref[4 + k] * quarter, quarter)
            part = ref[0, plane]
            a_ref[:, pl.ds(plane * frames + at, quarter)] = part
            if plane == 0:
                a_ref[:, pl.ds(2 * frames + at, quarter)] = -part
    size = a_ref.shape[0]
    b = b_ref[...].reshape(size, 2 * frames)
    scale = 1.0 / frames
    for plane in range(2):
        a = a_ref[:, plane * frames : (plane + 2) * frames]
        out_ref[0, plane] = (
            lax.dot_general(a, b, (((1,), (1,)), ((), ())), preferred_element_type=F32) * scale
        )


def correlate(order, cols, pieces, out, chunk, total):
    channels, _, size, quarter = pieces[0].shape
    _, _, chans, rows_of, frames = cols[0].shape
    col_spec = pl.BlockSpec((1, 2, chans, rows_of, frames), lambda k, s: (k, 0, 0, 0, 0))
    row_spec = pl.BlockSpec((1, 2, size, quarter), lambda k, s: (k, 0, 0, 0))
    in_specs = [col_spec] * 4 + [row_spec] * 4
    operands = [order, *cols, *pieces]
    aliases = {}
    if out is not None:
        in_specs.append(pl.BlockSpec(memory_space=pl.ANY))
        aliases = {len(operands): 0}
        operands.append(out)
    first = chunk * channels
    return pl.pallas_call(
        correlate_kernel,
        grid_spec=pltpu.PrefetchScalarGridSpec(
            num_scalar_prefetch=1,
            grid=(channels,),
            in_specs=in_specs,
            out_specs=pl.BlockSpec((1, 2, size, size), lambda k, s: (first + k, 0, 0, 0)),
            scratch_shapes=[
                pltpu.VMEM((size, 3 * frames), BF16),
                pltpu.VMEM((chans, 4, rows_of, 2 * frames), BF16),
            ],
        ),
        out_shape=jax.ShapeDtypeStruct((total, 2, size, size), F32),
        input_output_aliases=aliases,
        compiler_params=pltpu.CompilerParams(vmem_limit_bytes=48 << 20),
        cost_estimate=pl.CostEstimate(
            flops=8 * channels * size * size * frames,
            bytes_accessed=channels * (8 * size * frames + 8 * size * size),
            transcendentals=0,
        ),
        name="correlate",
    )(*operands)


def shards(voltages, window, kept_channels):
    chan_count = lax.axis_size("chan")
    row_count = lax.axis_size("row")
    col_count = 4
    points = window.shape[1]
    slots = voltages.shape[2]
    per_chan = kept_channels.shape[0] // chan_count
    hi, lo = phase_rows(kept_channels, points, chan_count, slots)
    sent = spectra(voltages, window, hi, lo, chan_count, col_count)
    kinds = per_chan // CHUNKS * 2
    me, far, near = (lax.axis_index(a) for a in ("row", "col_0", "col_1"))
    order = [(me + k) % row_count for k in (0, row_count - 1, 1, 2)]
    order += [f * 2 + n for f, n in ((far, near), (1 - far, near), (far, 1 - near), (1 - far, 1 - near))]
    order = jnp.stack(order).astype(jnp.int32)

    def turn(x, by):
        return lax.ppermute(x, "row", [(k, (k + by) % row_count) for k in range(row_count)])

    def swap(x, axis):
        return lax.ppermute(x, axis, [(0, 1), (1, 0)])

    cols, rows = [None] * CHUNKS, [None] * CHUNKS
    token = None
    for (kind, pieces), block in zip(STEPS, sent):
        axes = CHAN_COL if kind == "col" else CHAN_ROW_COL
        block = block.reshape(-1, *block.shape[-2:])
        if token is not None:
            block, token = lax.optimization_barrier((block, token))
        block = lax.all_to_all(block, axes, split_axis=0, concat_axis=0, tiled=True)
        block = regroup(block, kinds, slots)
        token = block[0]
        for piece, part in zip(pieces, block):
            if kind == "col":
                parts = [part, turn(part, 1), turn(part, -1), turn(part, 2)]
                parts = [c.reshape(kinds // 2, 2, chan_count, -1, c.shape[2]) for c in parts]
                cols[piece] = parts
            else:
                parts = [part, swap(part, "col_0")]
                parts += [swap(r, "col_1") for r in parts]
                rows[piece] = [r.reshape(kinds // 2, 2, *r.shape[1:]) for r in parts]
    out = None
    for chunk in range(CHUNKS):
        out = correlate(order, cols[chunk], rows[chunk], out, chunk, per_chan)
    return out


def solution(mesh):
    finer = Mesh(
        mesh.devices.reshape(mesh.shape["chan"], mesh.shape["row"], 2, 2),
        ("chan", "row", "col_0", "col_1"),
    )
    placed = (P(None, None, CHAN_ROW_COL, None, None), P(), P())
    return jax.shard_map(
        shards,
        mesh=finer,
        in_specs=placed,
        out_specs=P("chan", None, "row", ("col_0", "col_1")),
        check_vma=False,
    )
```

```python
import functools
import math

import jax
import jax.numpy as jnp
from jax import lax
from jax.experimental import pallas as pl
from jax.experimental.pallas import tpu as pltpu
from jax.sharding import Mesh
from jax.sharding import PartitionSpec as P

CHAN_COL = ("chan", "col_0", "col_1")
CHAN_ROW_COL = ("chan", "row", "col_0", "col_1")
CHUNKS = 2
STEPS = (("col", (0,)), ("row", (0, 1)), ("col", (1,)))
F32 = jnp.float32
BF16 = jnp.bfloat16


def split_bf16(x):
    hi = x.astype(BF16)
    return hi, (x - hi.astype(F32)).astype(BF16)


def phase_rows(kept_channels, points, chan_count, slots):
    positions = jnp.arange(points, dtype=jnp.int32)
    phases = kept_channels[:, None] * positions[None, :] % points
    angles = phases.astype(F32) * (2.0 * math.pi / points)
    factor = 1.0 / math.sqrt(points)
    cosines = jnp.cos(angles) * factor
    sines = jnp.sin(angles) * factor
    per_chan = kept_channels.shape[0] // chan_count
    real = jnp.concatenate([cosines, sines], axis=1)
    imag = jnp.concatenate([-sines, cosines], axis=1)
    rows = jnp.stack([real, imag], axis=1)
    rows = rows.reshape(chan_count, CHUNKS, per_chan // CHUNKS, 2, 2 * points)
    rows = rows.transpose(1, 0, 2, 3, 4).reshape(-1, 2 * points)
    eye = jnp.eye(slots, dtype=F32)
    blocks = rows[:, None, None, :] * eye[None, :, :, None]
    blocks = blocks.reshape(rows.shape[0] * slots, slots * 2 * points)
    near = lax.reduce_precision(blocks, 8, 7)
    return near.astype(BF16), (blocks - near).astype(BF16)


def spectra_kernel(volt_ref, win_ref, hi_ref, lo_ref, *refs):
    out_refs, part_ref = refs[:-1], refs[-1]
    slots, points, _ = volt_ref.shape[2:]
    frames = part_ref.shape[1]
    depth = slots * 2 * points
    group = 16
    steps = points // group

    def filter_rows(i, _):
        slot, plane, at = i // (2 * steps), i // steps % 2, i % steps * group
        x = volt_ref[plane, 0, slot, pl.ds(at, group), :]
        total = None
        for tap in range(win_ref.shape[0]):
            gain = win_ref[tap, pl.ds(at, group), :]
            gain = jnp.concatenate([gain] * (frames // 128), axis=1)
            term = gain * x[:, tap : tap + frames].astype(F32)
            total = term if total is None else total + term
        hi, lo = split_bf16(total)
        to = pl.multiple_of(i * group, group)
        part_ref[pl.ds(to, group)] = hi
        part_ref[pl.ds(to + depth, group)] = lo
        return 0

    lax.fori_loop(0, slots * 2 * steps, filter_rows, 0, unroll=32)
    out = jnp.dot(hi_ref[...], part_ref[0:depth], preferred_element_type=F32)
    out = out + jnp.dot(hi_ref[...], part_ref[depth:], preferred_element_type=F32)
    out = out + jnp.dot(lo_ref[...], part_ref[0:depth], preferred_element_type=F32)
    chans = out_refs[0].shape[0]
    out = out.astype(BF16).reshape(CHUNKS, chans, -1, frames)
    rows = out.shape[2]
    for (kind, pieces), ref in zip(STEPS, out_refs):
        for k, piece in enumerate(pieces):
            at = slice(k * rows, (k + 1) * rows)
            if kind == "col":
                ref[:, 0, at] = out[piece]
                continue
            quarter = ref.shape[4]
            for part in range(frames // quarter):
                ref[:, 0, part, at] = out[piece, :, :, part * quarter : (part + 1) * quarter]


def spectra(voltages, window, hi, lo, chan_count, col_count):
    _, panels, slots, points, blocks = voltages.shape
    taps = window.shape[0]
    frames = blocks - taps + 1
    rows = hi.shape[0] // (CHUNKS * chan_count)
    depth = hi.shape[1]
    width = pl.cdiv(blocks, 128) * 128
    window = jnp.broadcast_to(window[:, :, None], (taps, points, 128))
    quarter = frames // col_count
    specs, shapes = [], []
    for kind, pieces in STEPS:
        high = rows * len(pieces)
        inner = (high, frames) if kind == "col" else (col_count, high, quarter)
        zeros = (0,) * len(inner)
        specs.append(
            pl.BlockSpec((chan_count, 1, *inner), lambda p, zeros=zeros: (0, p, *zeros))
        )
        shapes.append(jax.ShapeDtypeStruct((chan_count, panels, *inner), BF16))
    return pl.pallas_call(
        spectra_kernel,
        grid=(panels,),
        in_specs=[
            pl.BlockSpec((2, 1, slots, points, width), lambda p: (0, p, 0, 0, 0)),
            pl.BlockSpec((taps, points, 128), lambda p: (0, 0, 0)),
            pl.BlockSpec(hi.shape, lambda p: (0, 0)),
            pl.BlockSpec(lo.shape, lambda p: (0, 0)),
        ],
        out_specs=specs,
        out_shape=shapes,
        scratch_shapes=[pltpu.VMEM((2 * depth, frames), BF16)],
        compiler_params=pltpu.CompilerParams(vmem_limit_bytes=48 << 20),
        name="spectra",
    )(voltages, window, hi, lo)


def regroup_kernel(size, slots, x_ref, *out_refs):
    kinds = out_refs[0].shape[0]
    total = kinds * len(out_refs)
    per = size // total
    rows = lax.broadcasted_iota(jnp.int32, (size, size), 0)
    cols = lax.broadcasted_iota(jnp.int32, (size, size), 1)
    kind, rest = rows // per, rows % per
    source = (rest // slots) * (total * slots) + kind * slots + rest % slots
    pick = (cols == source).astype(F32).astype(BF16)
    for g in range(x_ref.shape[0] // size):
        out = jnp.dot(
            pick, x_ref[g * size : (g + 1) * size], preferred_element_type=F32
        ).astype(BF16)
        out = out.reshape(total, per, -1)
        for k, ref in enumerate(out_refs):
            ref[:, g * per : (g + 1) * per] = out[k * kinds : (k + 1) * kinds]


def regroup(x, kinds, slots):
    count, rows, frames = x.shape
    pieces = rows // (kinds * slots)
    size = rows * (16 if pieces == 1 else 8)
    steps = 2
    part = count * rows // steps
    high = count * slots
    return pl.pallas_call(
        functools.partial(regroup_kernel, size, slots),
        grid=(steps,),
        in_specs=[pl.BlockSpec((part, frames), lambda g: (g, 0))],
        out_specs=[pl.BlockSpec((kinds, high // steps, frames), lambda g: (0, g, 0))] * pieces,
        out_shape=[jax.ShapeDtypeStruct((kinds, high, frames), BF16)] * pieces,
        cost_estimate=pl.CostEstimate(
            flops=2 * size * count * rows * frames,
            bytes_accessed=4 * count * rows * frames,
            transcendentals=0,
        ),
        compiler_params=pltpu.CompilerParams(vmem_limit_bytes=24 << 20),
        name="regroup",
    )(x.reshape(count * rows, frames))


def correlate_kernel(order_ref, *refs):
    cols, pieces = refs[0:5], refs[5:9]
    out_ref, a_ref, b_ref = refs[-3:]
    frames = cols[0].shape[4]
    quarter = pieces[0].shape[3]
    half = cols[3].shape[2]
    places = (slice(None), slice(None), slice(None), slice(0, half), slice(half, None))
    for plane in range(2):
        for k, (ref, place) in enumerate(zip(cols, places)):
            to = slice(plane * frames, (plane + 1) * frames)
            b_ref[place, order_ref[min(k, 3)], :, to] = ref[0, plane]
        for k, ref in enumerate(pieces):
            at = pl.multiple_of(order_ref[4 + k] * quarter, quarter)
            part = ref[0, plane]
            a_ref[:, pl.ds(plane * frames + at, quarter)] = part
            if plane == 0:
                a_ref[:, pl.ds(2 * frames + at, quarter)] = -part
    size = a_ref.shape[0]
    b = b_ref[...].reshape(size, 2 * frames)
    scale = 1.0 / frames
    for plane in range(2):
        a = a_ref[:, plane * frames : (plane + 2) * frames]
        out_ref[0, plane] = (
            lax.dot_general(a, b, (((1,), (1,)), ((), ())), preferred_element_type=F32) * scale
        )


def correlate(order, cols, pieces, out, first, total):
    channels, _, size, quarter = pieces[0].shape
    _, _, chans, rows_of, frames = cols[0].shape
    row_spec = pl.BlockSpec((1, 2, size, quarter), lambda k, s: (k, 0, 0, 0))
    in_specs = [
        pl.BlockSpec((1, *c.shape[1:]), lambda k, s: (k, 0, 0, 0, 0)) for c in cols
    ] + [row_spec] * 4
    operands = [order, *cols, *pieces]
    aliases = {}
    if out is not None:
        in_specs.append(pl.BlockSpec(memory_space=pl.ANY))
        aliases = {len(operands): 0}
        operands.append(out)
    return pl.pallas_call(
        correlate_kernel,
        grid_spec=pltpu.PrefetchScalarGridSpec(
            num_scalar_prefetch=1,
            grid=(channels,),
            in_specs=in_specs,
            out_specs=pl.BlockSpec((1, 2, size, size), lambda k, s: (first + k, 0, 0, 0)),
            scratch_shapes=[
                pltpu.VMEM((size, 3 * frames), BF16),
                pltpu.VMEM((chans, 4, rows_of, 2 * frames), BF16),
            ],
        ),
        out_shape=jax.ShapeDtypeStruct((total, 2, size, size), F32),
        input_output_aliases=aliases,
        compiler_params=pltpu.CompilerParams(vmem_limit_bytes=48 << 20),
        cost_estimate=pl.CostEstimate(
            flops=8 * channels * size * size * frames,
            bytes_accessed=channels * (8 * size * frames + 8 * size * size),
            transcendentals=0,
        ),
        name="correlate",
    )(*operands)


def shards(voltages, window, kept_channels):
    chan_count = lax.axis_size("chan")
    row_count = lax.axis_size("row")
    col_count = 4
    points = window.shape[1]
    slots = voltages.shape[2]
    per_chan = kept_channels.shape[0] // chan_count
    hi, lo = phase_rows(kept_channels, points, chan_count, slots)
    sent = spectra(voltages, window, hi, lo, chan_count, col_count)
    kinds = per_chan // CHUNKS * 2
    me, far, near = (lax.axis_index(a) for a in ("row", "col_0", "col_1"))
    order = [(me + k) % row_count for k in (0, row_count - 1, 1, 2)]
    order += [f * 2 + n for f, n in ((far, near), (1 - far, near), (far, 1 - near), (1 - far, 1 - near))]
    order = jnp.stack(order).astype(jnp.int32)

    def turn(x, by):
        return lax.ppermute(x, "row", [(k, (k + by) % row_count) for k in range(row_count)])

    def swap(x, axis):
        return lax.ppermute(x, axis, [(0, 1), (1, 0)])

    def after(x, *others):
        return lax.optimization_barrier((x, others))[0]

    def exchange(block, axes):
        block = block.reshape(-1, *block.shape[-2:])
        block = lax.all_to_all(block, axes, split_axis=0, concat_axis=0, tiled=True)
        return regroup(block, kinds, slots)

    def onward(up, down):
        half = up.shape[1] // 2
        return turn(up[:, :half], 1), turn(down[:, half:], -1)

    (first,) = exchange(sent[0], CHAN_COL)
    near_0 = turn(first, 1), turn(first, -1)
    rows = exchange(after(sent[1], first), CHAN_ROW_COL)
    rows = [(r, swap(r, "col_0")) for r in rows]
    (second,) = exchange(after(sent[2], *rows[0], *near_0), CHAN_COL)
    far_0 = onward(*near_0)
    second = after(second, *far_0)
    near_1 = turn(second, 1), turn(second, -1)
    cols = [(first, *near_0, *far_0), (second, *near_1, *onward(*near_1))]
    rows[1] = tuple(after(r, *near_1) for r in rows[1])
    rows = [(*r, *(swap(q, "col_1") for q in r)) for r in rows]
    cols = [[c.reshape(kinds // 2, 2, -1, 16, c.shape[2]) for c in p] for p in cols]
    rows = [[r.reshape(kinds // 2, 2, *r.shape[1:]) for r in p] for p in rows]
    out = None
    for chunk in range(CHUNKS):
        out = correlate(order, cols[chunk], rows[chunk], out, chunk * (kinds // 2), per_chan)
    return out


def solution(mesh):
    finer = Mesh(
        mesh.devices.reshape(mesh.shape["chan"], mesh.shape["row"], 2, 2),
        ("chan", "row", "col_0", "col_1"),
    )
    placed = (P(None, None, CHAN_ROW_COL, None, None), P(), P())
    return jax.shard_map(
        shards,
        mesh=finer,
        in_specs=placed,
        out_specs=P("chan", None, "row", ("col_0", "col_1")),
        check_vma=False,
    )
```

```python
import functools
import math

import jax
import jax.numpy as jnp
from jax import lax
from jax.experimental import pallas as pl
from jax.experimental.pallas import tpu as pltpu
from jax.sharding import Mesh
from jax.sharding import PartitionSpec as P

CHAN_COL = ("chan", "col_0", "col_1")
CHAN_ROW_COL = ("chan", "row", "col_0", "col_1")
CHUNKS = 2
STEPS = (("col", (0,)), ("row", (0, 1)), ("col", (1,)))
F32 = jnp.float32
BF16 = jnp.bfloat16


def split_bf16(x):
    hi = x.astype(BF16)
    return hi, (x - hi.astype(F32)).astype(BF16)


def phase_rows(kept_channels, points, chan_count, slots):
    positions = jnp.arange(points, dtype=jnp.int32)
    phases = kept_channels[:, None] * positions[None, :] % points
    angles = phases.astype(F32) * (2.0 * math.pi / points)
    factor = 1.0 / math.sqrt(points)
    cosines = jnp.cos(angles) * factor
    sines = jnp.sin(angles) * factor
    per_chan = kept_channels.shape[0] // chan_count
    real = jnp.concatenate([cosines, sines], axis=1)
    imag = jnp.concatenate([-sines, cosines], axis=1)
    rows = jnp.stack([real, imag], axis=1)
    rows = rows.reshape(chan_count, CHUNKS, per_chan // CHUNKS, 2, 2 * points)
    rows = rows.transpose(1, 0, 2, 3, 4).reshape(-1, 2 * points)
    eye = jnp.eye(slots, dtype=F32)
    blocks = rows[:, None, None, :] * eye[None, :, :, None]
    blocks = blocks.reshape(rows.shape[0] * slots, slots * 2 * points)
    near = lax.reduce_precision(blocks, 8, 7)
    return near.astype(BF16), (blocks - near).astype(BF16)


def spectra_kernel(volt_ref, win_ref, hi_ref, lo_ref, *refs):
    out_refs, part_ref = refs[:-1], refs[-1]
    slots, points, _ = volt_ref.shape[2:]
    frames = part_ref.shape[1]
    depth = slots * 2 * points
    group = 16
    steps = points // group

    def filter_rows(i, _):
        slot, plane, at = i // (2 * steps), i // steps % 2, i % steps * group
        x = volt_ref[plane, 0, slot, pl.ds(at, group), :]
        total = None
        for tap in range(win_ref.shape[0]):
            gain = win_ref[tap, pl.ds(at, group), :]
            gain = jnp.concatenate([gain] * (frames // 128), axis=1)
            term = gain * x[:, tap : tap + frames].astype(F32)
            total = term if total is None else total + term
        hi, lo = split_bf16(total)
        to = pl.multiple_of(i * group, group)
        part_ref[pl.ds(to, group)] = hi
        part_ref[pl.ds(to + depth, group)] = lo
        return 0

    lax.fori_loop(0, slots * 2 * steps, filter_rows, 0, unroll=32)
    out = jnp.dot(hi_ref[...], part_ref[0:depth], preferred_element_type=F32)
    out = out + jnp.dot(hi_ref[...], part_ref[depth:], preferred_element_type=F32)
    out = out + jnp.dot(lo_ref[...], part_ref[0:depth], preferred_element_type=F32)
    chans = out_refs[0].shape[0]
    out = out.astype(BF16).reshape(CHUNKS, chans, -1, frames)
    rows = out.shape[2]
    for (kind, pieces), ref in zip(STEPS, out_refs):
        for k, piece in enumerate(pieces):
            at = slice(k * rows, (k + 1) * rows)
            if kind == "col":
                ref[:, 0, at] = out[piece]
                continue
            quarter = ref.shape[4]
            for part in range(frames // quarter):
                ref[:, 0, part, at] = out[piece, :, :, part * quarter : (part + 1) * quarter]


def spectra(voltages, window, hi, lo, chan_count, col_count):
    _, panels, slots, points, blocks = voltages.shape
    taps = window.shape[0]
    frames = blocks - taps + 1
    rows = hi.shape[0] // (CHUNKS * chan_count)
    depth = hi.shape[1]
    width = pl.cdiv(blocks, 128) * 128
    window = jnp.broadcast_to(window[:, :, None], (taps, points, 128))
    quarter = frames // col_count
    specs, shapes = [], []
    for kind, pieces in STEPS:
        high = rows * len(pieces)
        inner = (high, frames) if kind == "col" else (col_count, high, quarter)
        zeros = (0,) * len(inner)
        specs.append(
            pl.BlockSpec((chan_count, 1, *inner), lambda p, zeros=zeros: (0, p, *zeros))
        )
        shapes.append(jax.ShapeDtypeStruct((chan_count, panels, *inner), BF16))
    return pl.pallas_call(
        spectra_kernel,
        grid=(panels,),
        in_specs=[
            pl.BlockSpec((2, 1, slots, points, width), lambda p: (0, p, 0, 0, 0)),
            pl.BlockSpec((taps, points, 128), lambda p: (0, 0, 0)),
            pl.BlockSpec(hi.shape, lambda p: (0, 0)),
            pl.BlockSpec(lo.shape, lambda p: (0, 0)),
        ],
        out_specs=specs,
        out_shape=shapes,
        scratch_shapes=[pltpu.VMEM((2 * depth, frames), BF16)],
        compiler_params=pltpu.CompilerParams(vmem_limit_bytes=48 << 20),
        name="spectra",
    )(voltages, window, hi, lo)


def regroup_kernel(size, slots, x_ref, *out_refs):
    kinds = out_refs[0].shape[0]
    total = kinds * len(out_refs)
    per = size // total
    rows = lax.broadcasted_iota(jnp.int32, (size, size), 0)
    cols = lax.broadcasted_iota(jnp.int32, (size, size), 1)
    kind, rest = rows // per, rows % per
    source = (rest // slots) * (total * slots) + kind * slots + rest % slots
    pick = (cols == source).astype(F32).astype(BF16)
    for g in range(x_ref.shape[0] // size):
        out = jnp.dot(
            pick, x_ref[g * size : (g + 1) * size], preferred_element_type=F32
        ).astype(BF16)
        out = out.reshape(total, per, -1)
        for k, ref in enumerate(out_refs):
            ref[:, g * per : (g + 1) * per] = out[k * kinds : (k + 1) * kinds]


def regroup(x, kinds, slots):
    count, rows, frames = x.shape
    pieces = rows // (kinds * slots)
    size = rows * (16 if pieces == 1 else 8)
    steps = 2
    part = count * rows // steps
    high = count * slots
    return pl.pallas_call(
        functools.partial(regroup_kernel, size, slots),
        grid=(steps,),
        in_specs=[pl.BlockSpec((part, frames), lambda g: (g, 0))],
        out_specs=[pl.BlockSpec((kinds, high // steps, frames), lambda g: (0, g, 0))] * pieces,
        out_shape=[jax.ShapeDtypeStruct((kinds, high, frames), BF16)] * pieces,
        cost_estimate=pl.CostEstimate(
            flops=2 * size * count * rows * frames,
            bytes_accessed=4 * count * rows * frames,
            transcendentals=0,
        ),
        compiler_params=pltpu.CompilerParams(vmem_limit_bytes=24 << 20),
        name="regroup",
    )(x.reshape(count * rows, frames))


def correlate_kernel(order_ref, *refs):
    cols, pieces = refs[0:5], refs[5:9]
    out_ref, a_ref, b_ref = refs[-3:]
    frames = cols[0].shape[4]
    quarter = pieces[0].shape[3]
    half = cols[3].shape[2]
    places = (slice(None), slice(None), slice(None), slice(0, half), slice(half, None))
    for plane in range(2):
        for k, (ref, place) in enumerate(zip(cols, places)):
            to = slice(plane * frames, (plane + 1) * frames)
            b_ref[place, order_ref[min(k, 3)], :, to] = ref[0, plane]
        for k, ref in enumerate(pieces):
            at = pl.multiple_of(order_ref[4 + k] * quarter, quarter)
            part = ref[0, plane]
            a_ref[:, pl.ds(plane * frames + at, quarter)] = part
            if plane == 0:
                a_ref[:, pl.ds(2 * frames + at, quarter)] = -part
    size = a_ref.shape[0]
    b = b_ref[...].reshape(size, 2 * frames)
    scale = 1.0 / frames
    for plane in range(2):
        a = a_ref[:, plane * frames : (plane + 2) * frames]
        out_ref[0, plane] = (
            lax.dot_general(a, b, (((1,), (1,)), ((), ())), preferred_element_type=F32) * scale
        )


def correlate(order, cols, pieces, out, first, total):
    channels, _, size, quarter = pieces[0].shape
    _, _, chans, rows_of, frames = cols[0].shape
    row_spec = pl.BlockSpec((1, 2, size, quarter), lambda k, s: (k, 0, 0, 0))
    in_specs = [
        pl.BlockSpec((1, *c.shape[1:]), lambda k, s: (k, 0, 0, 0, 0)) for c in cols
    ] + [row_spec] * 4
    operands = [order, *cols, *pieces]
    aliases = {}
    if out is not None:
        in_specs.append(pl.BlockSpec(memory_space=pl.ANY))
        aliases = {len(operands): 0}
        operands.append(out)
    return pl.pallas_call(
        correlate_kernel,
        grid_spec=pltpu.PrefetchScalarGridSpec(
            num_scalar_prefetch=1,
            grid=(channels,),
            in_specs=in_specs,
            out_specs=pl.BlockSpec((1, 2, size, size), lambda k, s: (first + k, 0, 0, 0)),
            scratch_shapes=[
                pltpu.VMEM((size, 3 * frames), BF16),
                pltpu.VMEM((chans, 4, rows_of, 2 * frames), BF16),
            ],
        ),
        out_shape=jax.ShapeDtypeStruct((total, 2, size, size), F32),
        input_output_aliases=aliases,
        compiler_params=pltpu.CompilerParams(vmem_limit_bytes=48 << 20),
        cost_estimate=pl.CostEstimate(
            flops=8 * channels * size * size * frames,
            bytes_accessed=channels * (8 * size * frames + 8 * size * size),
            transcendentals=0,
        ),
        name="correlate",
    )(*operands)


def shards(voltages, window, kept_channels):
    chan_count = lax.axis_size("chan")
    row_count = lax.axis_size("row")
    col_count = 4
    points = window.shape[1]
    slots = voltages.shape[2]
    per_chan = kept_channels.shape[0] // chan_count
    hi, lo = phase_rows(kept_channels, points, chan_count, slots)
    sent = spectra(voltages, window, hi, lo, chan_count, col_count)
    kinds = per_chan // CHUNKS * 2
    me, far, near = (lax.axis_index(a) for a in ("row", "col_0", "col_1"))
    order = [(me + k) % row_count for k in (0, row_count - 1, 1, 2)]
    order += [f * 2 + n for f, n in ((far, near), (1 - far, near), (far, 1 - near), (1 - far, 1 - near))]
    order = jnp.stack(order).astype(jnp.int32)

    def turn(x, by):
        return lax.ppermute(x, "row", [(k, (k + by) % row_count) for k in range(row_count)])

    def swap(x, axis):
        return lax.ppermute(x, axis, [(0, 1), (1, 0)])

    def after(x, *others):
        return lax.optimization_barrier((x, others))[0]

    def exchange(block, axes, *others):
        block = block.reshape(-1, *block.shape[-2:])
        block = lax.all_to_all(block, axes, split_axis=0, concat_axis=0, tiled=True)
        if others:
            block = after(block, *others)
        return regroup(block, kinds, slots)

    def onward(up, down):
        half = up.shape[1] // 2
        return turn(up[:, :half], 1), turn(down[:, half:], -1)

    (first,) = exchange(sent[0], CHAN_COL)
    near_0 = turn(first, 1), turn(first, -1)
    rows = exchange(after(sent[1], first), CHAN_ROW_COL)
    rows = [(r, swap(r, "col_0")) for r in rows]
    (second,) = exchange(after(sent[2], rows[0][0]), CHAN_COL, *near_0, rows[0][1])
    far_0 = onward(*near_0)
    near_1 = after(second, *far_0)
    near_1 = turn(near_1, 1), turn(near_1, -1)
    far_1 = onward(*near_1)
    cols = [(first, *near_0, *far_0), (second, *near_1, *far_1)]
    rows[1] = tuple(after(r, *near_1) for r in rows[1])
    rows = [(*r, *(swap(q, "col_1") for q in r)) for r in rows]
    cols = [[c.reshape(kinds // 2, 2, -1, 16, c.shape[2]) for c in p] for p in cols]
    rows = [[r.reshape(kinds // 2, 2, *r.shape[1:]) for r in p] for p in rows]
    out = None
    for chunk in range(CHUNKS):
        out = correlate(order, cols[chunk], rows[chunk], out, chunk * (kinds // 2), per_chan)
    return out


def solution(mesh):
    finer = Mesh(
        mesh.devices.reshape(mesh.shape["chan"], mesh.shape["row"], 2, 2),
        ("chan", "row", "col_0", "col_1"),
    )
    placed = (P(None, None, CHAN_ROW_COL, None, None), P(), P())
    return jax.shard_map(
        shards,
        mesh=finer,
        in_specs=placed,
        out_specs=P("chan", None, "row", ("col_0", "col_1")),
        check_vma=False,
    )
```

```python
import functools
import math

import jax
import jax.numpy as jnp
from jax import lax
from jax.experimental import pallas as pl
from jax.experimental.pallas import tpu as pltpu
from jax.sharding import Mesh
from jax.sharding import PartitionSpec as P

CHAN_COL = ("chan", "col_0", "col_1")
CHAN_ROW_COL = ("chan", "row", "col_0", "col_1")
CHUNKS = 2
STEPS = (("col", (0,)), ("row", (0, 1)), ("col", (1,)))
F32 = jnp.float32
BF16 = jnp.bfloat16


def split_bf16(x):
    hi = x.astype(BF16)
    return hi, (x - hi.astype(F32)).astype(BF16)


def phase_rows(kept_channels, points, chan_count, slots):
    positions = jnp.arange(points, dtype=jnp.int32)
    phases = kept_channels[:, None] * positions[None, :] % points
    angles = phases.astype(F32) * (2.0 * math.pi / points)
    factor = 1.0 / math.sqrt(points)
    cosines = jnp.cos(angles) * factor
    sines = jnp.sin(angles) * factor
    per_chan = kept_channels.shape[0] // chan_count
    real = jnp.concatenate([cosines, sines], axis=1)
    imag = jnp.concatenate([-sines, cosines], axis=1)
    rows = jnp.stack([real, imag], axis=1)
    rows = rows.reshape(chan_count, CHUNKS, per_chan // CHUNKS, 2, 2 * points)
    rows = rows.transpose(1, 0, 2, 3, 4).reshape(-1, 2 * points)
    eye = jnp.eye(slots, dtype=F32)
    blocks = rows[:, None, None, :] * eye[None, :, :, None]
    blocks = blocks.reshape(rows.shape[0] * slots, slots * 2 * points)
    near = lax.reduce_precision(blocks, 8, 7)
    return near.astype(BF16), (blocks - near).astype(BF16)


def spectra_kernel(volt_ref, win_ref, hi_ref, lo_ref, *refs):
    out_refs, part_ref = refs[:-1], refs[-1]
    slots, points, _ = volt_ref.shape[2:]
    frames = part_ref.shape[1]
    depth = slots * 2 * points
    group = 16
    steps = points // group

    def filter_rows(i, _):
        slot, plane, at = i // (2 * steps), i // steps % 2, i % steps * group
        x = volt_ref[plane, 0, slot, pl.ds(at, group), :]
        total = None
        for tap in range(win_ref.shape[0]):
            gain = win_ref[tap, pl.ds(at, group), :]
            gain = jnp.concatenate([gain] * (frames // 128), axis=1)
            term = gain * x[:, tap : tap + frames].astype(F32)
            total = term if total is None else total + term
        hi, lo = split_bf16(total)
        to = pl.multiple_of(i * group, group)
        part_ref[pl.ds(to, group)] = hi
        part_ref[pl.ds(to + depth, group)] = lo
        return 0

    lax.fori_loop(0, slots * 2 * steps, filter_rows, 0, unroll=32)
    out = jnp.dot(hi_ref[...], part_ref[0:depth], preferred_element_type=F32)
    out = out + jnp.dot(hi_ref[...], part_ref[depth:], preferred_element_type=F32)
    out = out + jnp.dot(lo_ref[...], part_ref[0:depth], preferred_element_type=F32)
    chans = out_refs[0].shape[0]
    out = out.astype(BF16).reshape(CHUNKS, chans, -1, frames)
    rows = out.shape[2]
    for (kind, pieces), ref in zip(STEPS, out_refs):
        for k, piece in enumerate(pieces):
            at = slice(k * rows, (k + 1) * rows)
            if kind == "col":
                ref[:, 0, at] = out[piece]
                continue
            quarter = ref.shape[4]
            for part in range(frames // quarter):
                ref[:, 0, part, at] = out[piece, :, :, part * quarter : (part + 1) * quarter]


def spectra(voltages, window, hi, lo, chan_count, col_count):
    _, panels, slots, points, blocks = voltages.shape
    taps = window.shape[0]
    frames = blocks - taps + 1
    rows = hi.shape[0] // (CHUNKS * chan_count)
    depth = hi.shape[1]
    width = pl.cdiv(blocks, 128) * 128
    window = jnp.broadcast_to(window[:, :, None], (taps, points, 128))
    quarter = frames // col_count
    specs, shapes = [], []
    for kind, pieces in STEPS:
        high = rows * len(pieces)
        inner = (high, frames) if kind == "col" else (col_count, high, quarter)
        zeros = (0,) * len(inner)
        specs.append(
            pl.BlockSpec((chan_count, 1, *inner), lambda p, zeros=zeros: (0, p, *zeros))
        )
        shapes.append(jax.ShapeDtypeStruct((chan_count, panels, *inner), BF16))
    return pl.pallas_call(
        spectra_kernel,
        grid=(panels,),
        in_specs=[
            pl.BlockSpec((2, 1, slots, points, width), lambda p: (0, p, 0, 0, 0)),
            pl.BlockSpec((taps, points, 128), lambda p: (0, 0, 0)),
            pl.BlockSpec(hi.shape, lambda p: (0, 0)),
            pl.BlockSpec(lo.shape, lambda p: (0, 0)),
        ],
        out_specs=specs,
        out_shape=shapes,
        scratch_shapes=[pltpu.VMEM((2 * depth, frames), BF16)],
        compiler_params=pltpu.CompilerParams(vmem_limit_bytes=48 << 20),
        name="spectra",
    )(voltages, window, hi, lo)


def regroup_kernel(size, slots, x_ref, *out_refs):
    kinds = out_refs[0].shape[0]
    total = kinds * len(out_refs)
    per = size // total
    rows = lax.broadcasted_iota(jnp.int32, (size, size), 0)
    cols = lax.broadcasted_iota(jnp.int32, (size, size), 1)
    kind, rest = rows // per, rows % per
    source = (rest // slots) * (total * slots) + kind * slots + rest % slots
    pick = (cols == source).astype(F32).astype(BF16)
    for g in range(x_ref.shape[0] // size):
        out = jnp.dot(
            pick, x_ref[g * size : (g + 1) * size], preferred_element_type=F32
        ).astype(BF16)
        out = out.reshape(total, per, -1)
        for k, ref in enumerate(out_refs):
            ref[:, g * per : (g + 1) * per] = out[k * kinds : (k + 1) * kinds]


def regroup(x, kinds, slots):
    count, rows, frames = x.shape
    pieces = rows // (kinds * slots)
    size = rows * (16 if pieces == 1 else 8)
    steps = 2
    part = count * rows // steps
    high = count * slots
    return pl.pallas_call(
        functools.partial(regroup_kernel, size, slots),
        grid=(steps,),
        in_specs=[pl.BlockSpec((part, frames), lambda g: (g, 0))],
        out_specs=[pl.BlockSpec((kinds, high // steps, frames), lambda g: (0, g, 0))] * pieces,
        out_shape=[jax.ShapeDtypeStruct((kinds, high, frames), BF16)] * pieces,
        cost_estimate=pl.CostEstimate(
            flops=2 * size * count * rows * frames,
            bytes_accessed=4 * count * rows * frames,
            transcendentals=0,
        ),
        compiler_params=pltpu.CompilerParams(vmem_limit_bytes=24 << 20),
        name="regroup",
    )(x.reshape(count * rows, frames))


def correlate_kernel(order_ref, *refs):
    cols, pieces = refs[0:5], refs[5:9]
    out_ref, a_ref, b_ref = refs[-3:]
    frames = cols[0].shape[4]
    quarter = pieces[0].shape[3]
    half = cols[3].shape[2]
    places = (slice(None), slice(None), slice(None), slice(0, half), slice(half, None))
    for plane in range(2):
        for k, (ref, place) in enumerate(zip(cols, places)):
            to = slice(plane * frames, (plane + 1) * frames)
            b_ref[place, order_ref[min(k, 3)], :, to] = ref[0, plane]
        for k, ref in enumerate(pieces):
            at = pl.multiple_of(order_ref[4 + k] * quarter, quarter)
            part = ref[0, plane]
            a_ref[:, pl.ds(plane * frames + at, quarter)] = part
    size = a_ref.shape[0]
    b = b_ref[...].reshape(size, 2 * frames)
    scale = 1.0 / frames

    def cross(x, y):
        return lax.dot_general(x, y, (((1,), (1,)), ((), ())), preferred_element_type=F32)

    out_ref[0, 0] = cross(a_ref[...], b) * scale
    imag = cross(a_ref[:, frames:], b[:, :frames]) - cross(a_ref[:, :frames], b[:, frames:])
    out_ref[0, 1] = imag * scale


def correlate(order, cols, pieces, out, first, total):
    channels, _, size, quarter = pieces[0].shape
    _, _, chans, rows_of, frames = cols[0].shape
    row_spec = pl.BlockSpec((1, 2, size, quarter), lambda k, s: (k, 0, 0, 0))
    in_specs = [
        pl.BlockSpec((1, *c.shape[1:]), lambda k, s: (k, 0, 0, 0, 0)) for c in cols
    ] + [row_spec] * 4
    operands = [order, *cols, *pieces]
    aliases = {}
    if out is not None:
        in_specs.append(pl.BlockSpec(memory_space=pl.ANY))
        aliases = {len(operands): 0}
        operands.append(out)
    return pl.pallas_call(
        correlate_kernel,
        grid_spec=pltpu.PrefetchScalarGridSpec(
            num_scalar_prefetch=1,
            grid=(channels,),
            in_specs=in_specs,
            out_specs=pl.BlockSpec((1, 2, size, size), lambda k, s: (first + k, 0, 0, 0)),
            scratch_shapes=[
                pltpu.VMEM((size, 2 * frames), BF16),
                pltpu.VMEM((chans, 4, rows_of, 2 * frames), BF16),
            ],
        ),
        out_shape=jax.ShapeDtypeStruct((total, 2, size, size), F32),
        input_output_aliases=aliases,
        compiler_params=pltpu.CompilerParams(vmem_limit_bytes=48 << 20),
        cost_estimate=pl.CostEstimate(
            flops=8 * channels * size * size * frames,
            bytes_accessed=channels * (8 * size * frames + 8 * size * size),
            transcendentals=0,
        ),
        name="correlate",
    )(*operands)


def shards(voltages, window, kept_channels):
    chan_count = lax.axis_size("chan")
    row_count = lax.axis_size("row")
    col_count = 4
    points = window.shape[1]
    slots = voltages.shape[2]
    per_chan = kept_channels.shape[0] // chan_count
    hi, lo = phase_rows(kept_channels, points, chan_count, slots)
    sent = spectra(voltages, window, hi, lo, chan_count, col_count)
    kinds = per_chan // CHUNKS * 2
    me, far, near = (lax.axis_index(a) for a in ("row", "col_0", "col_1"))
    order = [(me + k) % row_count for k in (0, row_count - 1, 1, 2)]
    order += [f * 2 + n for f, n in ((far, near), (1 - far, near), (far, 1 - near), (1 - far, 1 - near))]
    order = jnp.stack(order).astype(jnp.int32)

    def turn(x, by):
        return lax.ppermute(x, "row", [(k, (k + by) % row_count) for k in range(row_count)])

    def swap(x, axis):
        return lax.ppermute(x, axis, [(0, 1), (1, 0)])

    def after(x, *others):
        return lax.optimization_barrier((x, others))[0]

    def exchange(block, axes, *others):
        block = block.reshape(-1, *block.shape[-2:])
        block = lax.all_to_all(block, axes, split_axis=0, concat_axis=0, tiled=True)
        if others:
            block = after(block, *others)
        return regroup(block, kinds, slots)

    def onward(up, down):
        half = up.shape[1] // 2
        return turn(up[:, :half], 1), turn(down[:, half:], -1)

    (first,) = exchange(sent[0], CHAN_COL)
    near_0 = turn(first, 1), turn(first, -1)
    rows = exchange(after(sent[1], first), CHAN_ROW_COL)
    rows = [(r, swap(r, "col_0")) for r in rows]
    (second,) = exchange(after(sent[2], rows[0][0]), CHAN_COL, *near_0, rows[0][1])
    far_0 = onward(*near_0)
    near_1 = after(second, *far_0)
    near_1 = turn(near_1, 1), turn(near_1, -1)
    far_1 = onward(*near_1)
    cols = [(first, *near_0, *far_0), (second, *near_1, *far_1)]
    rows[1] = tuple(after(r, *near_1) for r in rows[1])
    rows = [(*r, *(swap(q, "col_1") for q in r)) for r in rows]
    cols = [[c.reshape(kinds // 2, 2, -1, 16, c.shape[2]) for c in p] for p in cols]
    rows = [[r.reshape(kinds // 2, 2, *r.shape[1:]) for r in p] for p in rows]
    out = None
    for chunk in range(CHUNKS):
        out = correlate(order, cols[chunk], rows[chunk], out, chunk * (kinds // 2), per_chan)
    return out


def solution(mesh):
    finer = Mesh(
        mesh.devices.reshape(mesh.shape["chan"], mesh.shape["row"], 2, 2),
        ("chan", "row", "col_0", "col_1"),
    )
    placed = (P(None, None, CHAN_ROW_COL, None, None), P(), P())
    return jax.shard_map(
        shards,
        mesh=finer,
        in_specs=placed,
        out_specs=P("chan", None, "row", ("col_0", "col_1")),
        check_vma=False,
    )
```
